768 devices in a mesh: sec: 2 (over y_lo), seq: 48 (over x, z), mp: 8 (over y_hi, core).
Axes of the slice: x: 4, y: 8 (y_hi: 4, y_lo: 2; y = y_hi * 2 + y_lo), z: 12, core: 2. Of those that a mesh axis runs over, the one named last changes fastest.
Arguments:
- queries: bfloat16 [12288, 2048], P(('sec', 'seq'), 'mp'), may hold values from -6 to 6
- keys_values: bfloat16 [2, 192, 2048], P(None, ('sec', 'seq'), 'mp'), may hold values from -6 to 6
- out_grad: bfloat16 [12288, 4096], P(('sec', 'seq'), 'mp'), may hold values from -6 to 6
- out_weight: bfloat16 [2048, 4096], P('mp'), may hold values from -0.125 to 0.125
- enc_len: int32 [2], replicated, may hold values from 48 to 96
- dec_len: int32 [2], replicated, may hold values from 1 to 6144
Outputs:
- query_grad: bfloat16 [12288, 2048], P(('sec', 'seq'), 'mp')
- key_value_grad: bfloat16 [2, 192, 2048], P(None, ('sec', 'seq'), 'mp')
The draws below stay inside these ranges and needn't reach their ends.
All inputs are finite; a program needn't handle non-finite values.
Results may differ from the reference program's by a relative error of at most 0.014.
Values may be sent and summed in bfloat16 or wider, within the bound.
No kernel may reach another device: no remote copies, remote signals or barrier semaphores. Data moves between devices by JAX's collectives and lax.ppermute only.
A program may use at most 32 MiB of HBM per device.

```python
import jax
import jax.numpy as jnp
from jax import lax

D = 4096
H = 8
DH = 256
SEQS = 2
TQ = 12288
SE = 192


def draw_queries(key, part):
    base = jnp.clip(jax.random.normal(jax.random.fold_in(key, 1), (TQ, H * DH), jnp.float32), -6.0, 6.0)
    return base.astype(jnp.bfloat16)


def draw_keys_values(key, part):
    base = jnp.clip(jax.random.normal(jax.random.fold_in(key, 2), (2, SE, H * DH), jnp.float32), -6.0, 6.0)
    return base.astype(jnp.bfloat16)


def levels(rng, dims, pieces, low, largest):
    def one(axis_at, shards_of):
        steps = jax.random.uniform(jax.random.fold_in(jax.random.fold_in(rng, 6), axis_at), (shards_of,), jnp.float32, low / len(pieces), largest / len(pieces))
        return jnp.repeat(jnp.exp(steps), dims[axis_at] // shards_of).reshape((-1,) + (1,) * (len(dims) - axis_at - 1))

    level = one(*pieces[0])
    for cut in pieces[1:]:
        level = level * one(*cut)
    return level


def scatter_about(rng, shape, scale, most, shards=(), held_as=jnp.bfloat16):
    loudness = levels(rng, shape, shards, -0.22, 0.18) if shards else 1.0
    array = jax.random.normal(rng, shape, jnp.float32) * scale * loudness
    return jnp.minimum(jnp.maximum(array, -most), most).astype(held_as)


def setup_inputs(seed: int = 0) -> dict:
    streams_of = jax.random.split(jax.random.key(seed), 7)
    return {
        "queries": draw_queries(jax.random.fold_in(streams_of[6], 71), 0),
        "keys_values": draw_keys_values(jax.random.fold_in(streams_of[6], 71), 0),
        "out_grad": scatter_about(streams_of[2], (TQ, D), 1.0, 6.0, ((0, 96), (1, 8))),
        "out_weight": scatter_about(streams_of[3], (H * DH, D), (H * DH) ** -0.5, 0.125, ((0, 8),)),
        "enc_len": jax.random.randint(streams_of[4], (SEQS,), max(2, SE // SEQS // 2), SE // SEQS + 1).astype(jnp.int32),
        "dec_len": jax.random.randint(streams_of[5], (SEQS,), 1, TQ // SEQS + 1).astype(jnp.int32),
    }


def reference(queries, keys_values, out_grad, out_weight, enc_len, dec_len):
    score_scale = DH ** -0.5
    total_q = queries.shape[0]
    total_k = keys_values.shape[1]
    per_query_seq = total_q // SEQS
    per_key_seq = total_k // SEQS
    query_pos = jnp.arange(total_q, dtype=jnp.int32)
    key_pos = jnp.arange(total_k, dtype=jnp.int32)
    query_seg = query_pos // per_query_seq
    key_seg = key_pos // per_key_seq
    key_valid = (key_pos % per_key_seq) < enc_len[key_seg]
    query_valid = (query_pos % per_query_seq) < dec_len[query_seg]
    allowed = (query_seg[:, None] == key_seg[None, :]) & key_valid[None, :]
    grad_heads = jnp.dot(out_grad, out_weight.T, preferred_element_type=jnp.float32).astype(jnp.bfloat16)
    grad_heads = jnp.where(query_valid[:, None], grad_heads, jnp.zeros_like(grad_heads))

    def one_head(head_index):
        first_col = head_index * DH
        q_head = lax.dynamic_slice_in_dim(queries, first_col, DH, 1)
        k_head = lax.dynamic_slice_in_dim(keys_values[0], first_col, DH, 1)
        v_head = lax.dynamic_slice_in_dim(keys_values[1], first_col, DH, 1)
        g_head = lax.dynamic_slice_in_dim(grad_heads, first_col, DH, 1)
        scores = jnp.dot(q_head, k_head.T, preferred_element_type=jnp.float32) * score_scale
        scores = jnp.where(allowed, scores, -1e30)
        row_max = jnp.max(scores, axis=1, keepdims=True)
        expo_terms = jnp.where(allowed, jnp.exp(scores - row_max), 0.0)
        log_total = row_max + jnp.log(jnp.sum(expo_terms, axis=1, keepdims=True))
        attn_prob = jnp.where(allowed, jnp.exp(scores - log_total), 0.0)
        attn_out = jnp.dot(attn_prob, v_head.astype(jnp.float32), precision=lax.Precision.HIGHEST)
        row_delta = jnp.sum(g_head.astype(jnp.float32) * attn_out, axis=1, keepdims=True)
        grad_prob = jnp.dot(g_head, v_head.T, preferred_element_type=jnp.float32)
        grad_score = (attn_prob * (grad_prob - row_delta)).astype(jnp.bfloat16)
        grad_query = (jnp.dot(grad_score, k_head, preferred_element_type=jnp.float32) * score_scale).astype(jnp.bfloat16)
        grad_key = (jnp.dot(grad_score.T, q_head, preferred_element_type=jnp.float32) * score_scale).astype(jnp.bfloat16)
        grad_value = jnp.dot(attn_prob.astype(jnp.bfloat16).T, g_head, preferred_element_type=jnp.float32).astype(jnp.bfloat16)
        return grad_query, grad_key, grad_value

    grad_query, grad_key, grad_value = lax.map(one_head, jnp.arange(H, dtype=jnp.int32))
    query_grad = jnp.transpose(grad_query, (1, 0, 2)).reshape(total_q, H * DH)
    key_grad = jnp.transpose(grad_key, (1, 0, 2)).reshape(total_k, H * DH)
    value_grad = jnp.transpose(grad_value, (1, 0, 2)).reshape(total_k, H * DH)
    return query_grad, jnp.stack([key_grad, value_grad])
```

```python
import jax
import jax.numpy as jnp
from jax import lax
from jax.experimental import pallas as pl
from jax.experimental.pallas import tpu as pltpu
from jax.sharding import Mesh, PartitionSpec as P

DH = 256
SEQS = 2
F32 = jnp.float32
BF16 = jnp.bfloat16
VMEM = pl.BlockSpec(memory_space=pltpu.VMEM)
SMEM = pl.BlockSpec(memory_space=pltpu.SMEM)
PARAMS = pltpu.CompilerParams(vmem_limit_bytes=32 * 1024 * 1024)


def dot_nt(a, b):
    return lax.dot_general(a, b, (((1,), (1,)), ((), ())), preferred_element_type=F32)


def dot_tn(a, b):
    return lax.dot_general(a, b, (((0,), (0,)), ((), ())), preferred_element_type=F32)


def masked_softmax(scores, allowed):
    scores = jnp.where(allowed, scores, -1e30)
    expo = jnp.where(allowed, jnp.exp(scores - jnp.max(scores, axis=1, keepdims=True)), 0.0)
    return expo / jnp.sum(expo, axis=1, keepdims=True)


def project(og_ref, w_ref, core):
    chips, rows, slab = og_ref.shape
    total = jnp.zeros((rows, DH), F32)
    for chip in range(chips):
        first = pl.multiple_of((2 * chip + core) * slab, slab)
        total += dot_nt(og_ref[chip], w_ref[:, pl.ds(first, slab)])
    return total


def before_kernel(nums_ref, og_ref, w_ref, q_ref, kv_ref, part_ref, pk_ref, pv_ref, sw_ref, *, own):
    rows = og_ref.shape[1]
    total = kv_ref.shape[0]
    enc_limit = nums_ref[0]
    part_ref[...] = project(og_ref, w_ref, nums_ref[2])
    q = q_ref[...]
    kv = kv_ref[...]
    r = lax.broadcasted_iota(jnp.int32, (total, total), 0)
    c = lax.broadcasted_iota(jnp.int32, (total, total), 1)
    partner = jnp.where((r % (2 * own)) < own, r + own, r - own)
    swap = jnp.where(c == partner, 1.0, 0.0).astype(BF16)
    swapped = jnp.dot(swap, kv, preferred_element_type=F32).astype(BF16)
    sw_ref[...] = swapped
    scale = DH ** (-0.5)
    col = lax.broadcasted_iota(jnp.int32, (rows, total), 1)
    is_key = (col % (2 * own)) < own
    inside = (col // (2 * own)) * own + col % own < enc_limit
    pk_ref[...] = masked_softmax(dot_nt(q, kv) * scale, is_key & inside)
    pv_ref[...] = masked_softmax(
        dot_nt(q, swapped) * scale, jnp.logical_not(is_key) & inside
    ).astype(BF16)


def after_kernel(
    nums_ref, og_ref, w_ref, q_ref, kv_ref, part_ref, pk_ref, pv_ref, sw_ref, dq_ref, panel_ref
):
    rows = og_ref.shape[1]
    scale = DH ** (-0.5)
    grad = part_ref[...] + project(og_ref, w_ref, 1 - nums_ref[2])
    row = lax.broadcasted_iota(jnp.int32, (rows, DH), 0)
    g = jnp.where(row < nums_ref[1], grad, 0.0).astype(BF16)
    prob = pk_ref[...]
    grad_prob = dot_nt(g, sw_ref[...])
    delta = jnp.sum(prob * grad_prob, axis=1, keepdims=True)
    grad_score = (prob * (grad_prob - delta)).astype(BF16)
    panel = dot_tn(grad_score, q_ref[...]) * scale + dot_tn(pv_ref[...], g)
    panel_ref[...] = panel.astype(BF16)
    dq_ref[...] = (jnp.dot(grad_score, kv_ref[...], preferred_element_type=F32) * scale).astype(BF16)


def sum_kernel(parts_ref, out_ref):
    out_ref[...] = jnp.sum(parts_ref[...].astype(F32), axis=0).astype(BF16)


def body(queries, keys_values, out_grad, out_weight, enc_len, dec_len):
    rows = queries.shape[0]
    own = keys_values.shape[1]
    seq = ("sx", "sz")
    groups = lax.axis_size(seq)
    total = 2 * own * groups
    sec = lax.axis_index("sec")
    nums = jnp.stack(
        [enc_len[sec], dec_len[sec] - lax.axis_index(seq) * rows, lax.axis_index("mc")]
    )
    kv_mine = keys_values.reshape(1, 2 * own, DH)
    kv = lax.all_to_all(
        jnp.broadcast_to(kv_mine, (groups, 2 * own, DH)), seq, 0, 0, tiled=True
    ).reshape(total, DH)
    og, kv = lax.optimization_barrier((lax.all_gather(out_grad, "my", axis=0), kv))
    og_other = lax.ppermute(og, "mc", [(0, 1), (1, 0)])
    before = pl.pallas_call(
        lambda *refs: before_kernel(*refs, own=own),
        name="softmax_and_own_columns",
        out_shape=(
            jax.ShapeDtypeStruct((rows, DH), F32),
            jax.ShapeDtypeStruct((rows, total), F32),
            jax.ShapeDtypeStruct((rows, total), BF16),
            jax.ShapeDtypeStruct((total, DH), BF16),
        ),
        in_specs=[SMEM, VMEM, VMEM, VMEM, VMEM],
        out_specs=(VMEM,) * 4,
        compiler_params=PARAMS,
    )(nums, og, out_weight, queries, kv)
    query_grad, panel = pl.pallas_call(
        after_kernel,
        name="gradients",
        out_shape=(
            jax.ShapeDtypeStruct((rows, DH), BF16),
            jax.ShapeDtypeStruct((total, DH), BF16),
        ),
        in_specs=[SMEM] + [VMEM] * 8,
        out_specs=(VMEM, VMEM),
        compiler_params=PARAMS,
    )(nums, og_other, out_weight, queries, kv, *before)
    parts = lax.all_to_all(panel.reshape(groups, 2 * own, DH), seq, 0, 0, tiled=True)
    owned = pl.pallas_call(
        sum_kernel,
        name="sum_of_parts",
        out_shape=jax.ShapeDtypeStruct((2 * own, DH), BF16),
        in_specs=[VMEM],
        out_specs=VMEM,
        compiler_params=PARAMS,
    )(parts)
    return query_grad, owned.reshape(2, own, DH)


def solution(mesh):
    sizes = dict(mesh.shape)
    fine = Mesh(
        mesh.devices.reshape(sizes["sec"], 4, sizes["seq"] // 4, sizes["mp"] // 2, 2),
        ("sec", "sx", "sz", "my", "mc"),
    )
    tok, mp = ("sec", "sx", "sz"), ("my", "mc")
    return jax.shard_map(
        body,
        mesh=fine,
        in_specs=(P(tok, mp), P(None, tok, mp), P(tok, mp), P(mp, None), P(), P()),
        out_specs=(P(tok, mp), P(None, tok, mp)),
        check_vma=False,
    )
```

```python
import jax
import jax.numpy as jnp
from jax import lax
from jax.experimental import pallas as pl
from jax.experimental.pallas import tpu as pltpu
from jax.sharding import Mesh, PartitionSpec as P

DH = 256
SEQS = 2
F32 = jnp.float32
BF16 = jnp.bfloat16
VMEM = pl.BlockSpec(memory_space=pltpu.VMEM)
HBM = pl.BlockSpec(memory_space=pltpu.HBM)
PARAMS = pltpu.CompilerParams(vmem_limit_bytes=32 * 1024 * 1024)


def dot_nt(a, b):
    return lax.dot_general(a, b, (((1,), (1,)), ((), ())), preferred_element_type=F32)


def dot_tn(a, b):
    return lax.dot_general(a, b, (((0,), (0,)), ((), ())), preferred_element_type=F32)


def masked_softmax(scores, allowed):
    scores = jnp.where(allowed, scores, -1e30)
    expo = jnp.where(allowed, jnp.exp(scores - jnp.max(scores, axis=1, keepdims=True)), 0.0)
    return expo / jnp.sum(expo, axis=1, keepdims=True)


def project(og_ref, w_ref, core):
    chips, rows, slab = og_ref.shape
    total = jnp.zeros((rows, DH), F32)
    for chip in range(chips):
        first = pl.multiple_of((2 * chip + core) * slab, slab)
        total += dot_nt(og_ref[chip], w_ref[:, pl.ds(first, slab)])
    return total


def before_kernel(
    enc_hbm, dec_hbm, w_hbm, q_hbm, og_ref, kv_ref,
    w_ref, q_ref, part_ref, mask_ref, pk_ref, pv_ref, sw_ref,
    enc_ref, dec_ref, sems, *, own,
):
    copies = [
        pltpu.make_async_copy(src, dst, sems.at[i])
        for i, (src, dst) in enumerate(
            ((enc_hbm, enc_ref), (dec_hbm, dec_ref), (q_hbm, q_ref), (w_hbm, w_ref))
        )
    ]
    for copy in copies:
        copy.start()
    rows, total = pk_ref.shape
    sec = lax.axis_index("sec")
    kv = kv_ref[...]
    r = lax.broadcasted_iota(jnp.int32, (total, total), 0)
    c = lax.broadcasted_iota(jnp.int32, (total, total), 1)
    partner = jnp.where((r % (2 * own)) < own, r + own, r - own)
    swap = jnp.where(c == partner, 1.0, 0.0).astype(BF16)
    swapped = jnp.dot(swap, kv, preferred_element_type=F32).astype(BF16)
    sw_ref[...] = swapped
    scale = DH ** (-0.5)
    for copy in copies[:3]:
        copy.wait()
    q = q_ref[...]
    enc_limit = enc_ref[sec]
    col = lax.broadcasted_iota(jnp.int32, (rows, total), 1)
    is_key = (col % (2 * own)) < own
    inside = (col // (2 * own)) * own + col % own < enc_limit
    pk_ref[...] = masked_softmax(dot_nt(q, kv) * scale, is_key & inside)
    pv_ref[...] = masked_softmax(
        dot_nt(q, swapped) * scale, jnp.logical_not(is_key) & inside
    ).astype(BF16)
    valid_rows = dec_ref[sec] - lax.axis_index(("sx", "sz")) * rows
    row = lax.broadcasted_iota(jnp.int32, (rows, DH), 0)
    mask_ref[...] = jnp.where(row < valid_rows, 1.0, 0.0)
    copies[3].wait()
    part_ref[...] = project(og_ref, w_ref, lax.axis_index("mc"))


def after_kernel(
    og_ref, kv_ref, w_ref, q_ref, part_ref, mask_ref, pk_ref, pv_ref, sw_ref, dq_ref, panel_ref
):
    scale = DH ** (-0.5)
    grad = part_ref[...] + project(og_ref, w_ref, 1 - lax.axis_index("mc"))
    g = jnp.where(mask_ref[...] > 0.0, grad, 0.0).astype(BF16)
    prob = pk_ref[...]
    grad_prob = dot_nt(g, sw_ref[...])
    delta = jnp.sum(prob * grad_prob, axis=1, keepdims=True)
    grad_score = (prob * (grad_prob - delta)).astype(BF16)
    panel = dot_tn(grad_score, q_ref[...]) * scale + dot_tn(pv_ref[...], g)
    panel_ref[...] = panel.astype(BF16)
    dq_ref[...] = (jnp.dot(grad_score, kv_ref[...], preferred_element_type=F32) * scale).astype(BF16)


def sum_kernel(parts_ref, out_ref):
    total = jnp.sum(parts_ref[...].astype(F32), axis=0).astype(BF16)
    own = out_ref.shape[1]
    out_ref[0] = total[:own]
    out_ref[1] = total[own:]


def body(queries, keys_values, out_grad, out_weight, enc_len, dec_len):
    rows = queries.shape[0]
    own = keys_values.shape[1]
    seq = ("sx", "sz")
    groups = lax.axis_size(seq)
    total = 2 * own * groups
    kv = lax.all_to_all(
        jnp.broadcast_to(keys_values[None], (groups, 2, own, DH)), seq, 0, 0, tiled=True
    ).reshape(total, DH)
    og, kv = lax.optimization_barrier((lax.all_gather(out_grad, "my", axis=0), kv))
    og_other = lax.ppermute(og, "mc", [(0, 1), (1, 0)])
    kept = pl.pallas_call(
        lambda *refs: before_kernel(*refs, own=own),
        name="softmax_and_own_columns",
        out_shape=(
            jax.ShapeDtypeStruct(out_weight.shape, BF16),
            jax.ShapeDtypeStruct((rows, DH), BF16),
            jax.ShapeDtypeStruct((rows, DH), F32),
            jax.ShapeDtypeStruct((rows, DH), F32),
            jax.ShapeDtypeStruct((rows, total), F32),
            jax.ShapeDtypeStruct((rows, total), BF16),
            jax.ShapeDtypeStruct((total, DH), BF16),
        ),
        in_specs=[HBM] * 4 + [VMEM] * 2,
        out_specs=(VMEM,) * 7,
        scratch_shapes=[
            pltpu.SMEM(enc_len.shape, jnp.int32),
            pltpu.SMEM(dec_len.shape, jnp.int32),
            pltpu.SemaphoreType.DMA((4,)),
        ],
        compiler_params=PARAMS,
    )(enc_len, dec_len, out_weight, queries, og, kv)
    query_grad, panel = pl.pallas_call(
        after_kernel,
        name="gradients",
        out_shape=(
            jax.ShapeDtypeStruct((rows, DH), BF16),
            jax.ShapeDtypeStruct((total, DH), BF16),
        ),
        in_specs=[VMEM] * 9,
        out_specs=(VMEM, VMEM),
        compiler_params=PARAMS,
    )(og_other, kv, *kept)
    parts = lax.all_to_all(panel.reshape(groups, 2 * own, DH), seq, 0, 0, tiled=True)
    owned = pl.pallas_call(
        sum_kernel,
        name="sum_of_parts",
        out_shape=jax.ShapeDtypeStruct((2, own, DH), BF16),
        in_specs=[VMEM],
        out_specs=VMEM,
        compiler_params=PARAMS,
    )(parts)
    return query_grad, owned


def solution(mesh):
    sizes = dict(mesh.shape)
    fine = Mesh(
        mesh.devices.reshape(sizes["sec"], 4, sizes["seq"] // 4, sizes["mp"] // 2, 2),
        ("sec", "sx", "sz", "my", "mc"),
    )
    tok, mp = ("sec", "sx", "sz"), ("my", "mc")
    return jax.shard_map(
        body,
        mesh=fine,
        in_specs=(P(tok, mp), P(None, tok, mp), P(tok, mp), P(mp, None), P(), P()),
        out_specs=(P(tok, mp), P(None, tok, mp)),
        check_vma=False,
    )
```

```python
import jax
import jax.numpy as jnp
from jax import lax
from jax.experimental import pallas as pl
from jax.experimental.pallas import tpu as pltpu
from jax.sharding import Mesh, PartitionSpec as P

DH = 256
SEQS = 2
F32 = jnp.float32
BF16 = jnp.bfloat16
VMEM = pl.BlockSpec(memory_space=pltpu.VMEM)
HBM = pl.BlockSpec(memory_space=pltpu.HBM)
PARAMS = pltpu.CompilerParams(vmem_limit_bytes=32 * 1024 * 1024)


def dot_nt(a, b):
    return lax.dot_general(a, b, (((1,), (1,)), ((), ())), preferred_element_type=F32)


def dot_tn(a, b):
    return lax.dot_general(a, b, (((0,), (0,)), ((), ())), preferred_element_type=F32)


def masked_softmax(scores, allowed):
    scores = jnp.where(allowed, scores, -1e30)
    expo = jnp.where(allowed, jnp.exp(scores - jnp.max(scores, axis=1, keepdims=True)), 0.0)
    return expo / jnp.sum(expo, axis=1, keepdims=True)


def project(og_ref, w_ref, core):
    chips, rows, slab = og_ref.shape
    total = jnp.zeros((rows, DH), F32)
    for chip in range(chips):
        first = pl.multiple_of((2 * chip + core) * slab, slab)
        total += dot_nt(og_ref[chip], w_ref[:, pl.ds(first, slab)])
    return total


def before_kernel(
    enc_hbm, dec_hbm, w_hbm, q_hbm, og_ref, kv_ref,
    w_ref, q_ref, part_ref, mask_ref, pk_ref, pv_ref, sw_ref,
    enc_ref, dec_ref, sems, *, own,
):
    copies = [
        pltpu.make_async_copy(src, dst, sems.at[i])
        for i, (src, dst) in enumerate(
            ((enc_hbm, enc_ref), (dec_hbm, dec_ref), (q_hbm, q_ref), (w_hbm, w_ref))
        )
    ]
    for copy in copies:
        copy.start()
    rows, total = pk_ref.shape
    sec = lax.axis_index("sec")
    kv = kv_ref[...]
    r = lax.broadcasted_iota(jnp.int32, (total, total), 0)
    c = lax.broadcasted_iota(jnp.int32, (total, total), 1)
    partner = jnp.where((r % (2 * own)) < own, r + own, r - own)
    swap = jnp.where(c == partner, 1.0, 0.0).astype(BF16)
    swapped = jnp.dot(swap, kv, preferred_element_type=F32).astype(BF16)
    sw_ref[...] = swapped
    scale = DH ** (-0.5)
    for copy in copies[:3]:
        copy.wait()
    q = q_ref[...]
    enc_limit = enc_ref[sec]
    col = lax.broadcasted_iota(jnp.int32, (rows, total), 1)
    is_key = (col % (2 * own)) < own
    inside = (col // (2 * own)) * own + col % own < enc_limit
    pk_ref[...] = masked_softmax(dot_nt(q, kv) * scale, is_key & inside)
    pv_ref[...] = masked_softmax(
        dot_nt(q, swapped) * scale, jnp.logical_not(is_key) & inside
    ).astype(BF16)
    valid_rows = dec_ref[sec] - lax.axis_index(("sx", "sz")) * rows
    row = lax.broadcasted_iota(jnp.int32, (rows, DH), 0)
    mask_ref[...] = jnp.where(row < valid_rows, 1.0, 0.0)
    copies[3].wait()
    part_ref[...] = project(og_ref, w_ref, lax.axis_index("mc"))


def after_kernel(
    og_ref, kv_ref, w_ref, q_ref, part_ref, mask_ref, pk_ref, pv_ref, sw_ref, dq_ref, panel_ref
):
    scale = DH ** (-0.5)
    grad = part_ref[...] + project(og_ref, w_ref, 1 - lax.axis_index("mc"))
    g = jnp.where(mask_ref[...] > 0.0, grad, 0.0).astype(BF16)
    prob = pk_ref[...]
    grad_prob = dot_nt(g, sw_ref[...])
    delta = jnp.sum(prob * grad_prob, axis=1, keepdims=True)
    grad_score = (prob * (grad_prob - delta)).astype(BF16)
    panel = dot_tn(grad_score, q_ref[...]) * scale + dot_tn(pv_ref[...], g)
    panel_ref[...] = panel.astype(BF16)
    dq_ref[...] = (jnp.dot(grad_score, kv_ref[...], preferred_element_type=F32) * scale).astype(BF16)


def sum_kernel(parts_ref, out_ref):
    total = jnp.sum(parts_ref[...].astype(F32), axis=0).astype(BF16)
    own = out_ref.shape[1]
    out_ref[0] = total[:own]
    out_ref[1] = total[own:]


def in_hbm(x):
    return pltpu.with_memory_space_constraint(x, pltpu.HBM)


def body(queries, keys_values, out_grad, out_weight, enc_len, dec_len):
    rows = queries.shape[0]
    own = keys_values.shape[1]
    seq = ("sx", "sz")
    groups = lax.axis_size(seq)
    total = 2 * own * groups
    kv = lax.all_to_all(
        jnp.broadcast_to(keys_values[None], (groups, 2, own, DH)), seq, 0, 0, tiled=True
    ).reshape(total, DH)
    og, kv = lax.optimization_barrier((lax.all_gather(out_grad, "my", axis=0), kv))
    og_other = lax.ppermute(og, "mc", [(0, 1), (1, 0)])
    kept = pl.pallas_call(
        lambda *refs: before_kernel(*refs, own=own),
        name="softmax_and_own_columns",
        out_shape=(
            jax.ShapeDtypeStruct(out_weight.shape, BF16),
            jax.ShapeDtypeStruct((rows, DH), BF16),
            jax.ShapeDtypeStruct((rows, DH), F32),
            jax.ShapeDtypeStruct((rows, DH), F32),
            jax.ShapeDtypeStruct((rows, total), F32),
            jax.ShapeDtypeStruct((rows, total), BF16),
            jax.ShapeDtypeStruct((total, DH), BF16),
        ),
        in_specs=[HBM] * 4 + [VMEM] * 2,
        out_specs=(VMEM,) * 7,
        scratch_shapes=[
            pltpu.SMEM(enc_len.shape, jnp.int32),
            pltpu.SMEM(dec_len.shape, jnp.int32),
            pltpu.SemaphoreType.DMA((4,)),
        ],
        compiler_params=PARAMS,
    )(*map(in_hbm, (enc_len, dec_len, out_weight, queries)), og, kv)
    query_grad, panel = pl.pallas_call(
        after_kernel,
        name="gradients",
        out_shape=(
            jax.ShapeDtypeStruct((rows, DH), BF16),
            jax.ShapeDtypeStruct((total, DH), BF16),
        ),
        in_specs=[VMEM] * 9,
        out_specs=(VMEM, VMEM),
        compiler_params=PARAMS,
    )(og_other, kv, *kept)
    parts = lax.all_to_all(panel.reshape(groups, 2 * own, DH), seq, 0, 0, tiled=True)
    owned = pl.pallas_call(
        sum_kernel,
        name="sum_of_parts",
        out_shape=jax.ShapeDtypeStruct((2, own, DH), BF16),
        in_specs=[VMEM],
        out_specs=VMEM,
        compiler_params=PARAMS,
    )(parts)
    return query_grad, owned


def solution(mesh):
    sizes = dict(mesh.shape)
    fine = Mesh(
        mesh.devices.reshape(sizes["sec"], 4, sizes["seq"] // 4, sizes["mp"] // 2, 2),
        ("sec", "sx", "sz", "my", "mc"),
    )
    tok, mp = ("sec", "sx", "sz"), ("my", "mc")
    return jax.shard_map(
        body,
        mesh=fine,
        in_specs=(P(tok, mp), P(None, tok, mp), P(tok, mp), P(mp, None), P(), P()),
        out_specs=(P(tok, mp), P(None, tok, mp)),
        check_vma=False,
    )
```

```python
import jax
import jax.numpy as jnp
from jax import lax
from jax.experimental import pallas as pl
from jax.experimental.pallas import tpu as pltpu
from jax.sharding import Mesh, PartitionSpec as P

DH = 256
F32 = jnp.float32
BF16 = jnp.bfloat16
VMEM = pl.BlockSpec(memory_space=pltpu.VMEM)
HBM = pl.BlockSpec(memory_space=pltpu.HBM)
PARAMS = pltpu.CompilerParams(vmem_limit_bytes=32 * 1024 * 1024)
KV_FIRST = 24
SUM_FIRST = 30


def dot_nt(a, b):
    return lax.dot_general(a, b, (((1,), (1,)), ((), ())), preferred_element_type=F32)


def dot_tn(a, b):
    return lax.dot_general(a, b, (((0,), (0,)), ((), ())), preferred_element_type=F32)


def masked_softmax(scores, allowed):
    scores = jnp.where(allowed, scores, -1e30)
    expo = jnp.where(allowed, jnp.exp(scores - jnp.max(scores, axis=1, keepdims=True)), 0.0)
    return expo / jnp.sum(expo, axis=1, keepdims=True)


def project(og_ref, w_ref, core):
    chips, rows, slab = og_ref.shape
    total = jnp.zeros((rows, DH), F32)
    for chip in range(chips):
        first = pl.multiple_of((2 * chip + core) * slab, slab)
        total += dot_nt(og_ref[chip], w_ref[:, pl.ds(first, slab)])
    return total


def swap_keys_values(kv, own):
    total = kv.shape[0]
    r = lax.broadcasted_iota(jnp.int32, (total, total), 0)
    c = lax.broadcasted_iota(jnp.int32, (total, total), 1)
    partner = jnp.where((r % (2 * own)) < own, r + own, r - own)
    swap = jnp.where(c == partner, 1.0, 0.0).astype(BF16)
    return jnp.dot(swap, kv, preferred_element_type=F32).astype(BF16)


def probabilities(q, kv, swapped, enc_limit, own):
    rows, total = q.shape[0], kv.shape[0]
    peers = total // (2 * own)
    scale = DH ** (-0.5)
    col = lax.broadcasted_iota(jnp.int32, (rows, total), 1)
    is_key = (col % (2 * own)) < own
    peer = (col // (2 * own) + KV_FIRST) % peers
    inside = peer * own + col % own < enc_limit
    at_keys = masked_softmax(dot_nt(q, kv) * scale, is_key & inside)
    at_values = masked_softmax(dot_nt(q, swapped) * scale, jnp.logical_not(is_key) & inside)
    return at_keys, at_values.astype(BF16)


def gradients(g, q, kv, swapped, prob, prob_v, dq_ref, panel_ref, own):
    scale = DH ** (-0.5)
    grad_prob = dot_nt(g, swapped)
    delta = jnp.sum(prob * grad_prob, axis=1, keepdims=True)
    grad_score = (prob * (grad_prob - delta)).astype(BF16)
    panel = dot_tn(grad_score, q) * scale + dot_tn(prob_v, g)
    peers = panel.shape[0] // (2 * own)
    shift = ((SUM_FIRST - KV_FIRST) % peers) * 2 * own
    if shift:
        panel = jnp.concatenate([panel[shift:], panel[:shift]], axis=0)
    panel_ref[...] = panel.astype(BF16)
    dq_ref[...] = (jnp.dot(grad_score, kv, preferred_element_type=F32) * scale).astype(BF16)


def sum_kernel(parts_ref, out_ref):
    total = jnp.sum(parts_ref[...].astype(F32), axis=0).astype(BF16)
    own = out_ref.shape[1]
    out_ref[0] = total[:own]
    out_ref[1] = total[own:]


def in_hbm(x):
    return pltpu.with_memory_space_constraint(x, pltpu.HBM)


def exchange(x, first):
    peers = x.shape[0]
    order = [(first + i) % peers for i in range(peers)]
    return lax.all_to_all(x, "seq", 0, 0, tiled=True, axis_index_groups=[order])


def sum_over_seq(panel, groups, own):
    parts = exchange(panel.reshape(groups, 2 * own, DH), SUM_FIRST)
    return pl.pallas_call(
        sum_kernel,
        name="sum_of_parts",
        out_shape=jax.ShapeDtypeStruct((2, own, DH), BF16),
        in_specs=[VMEM],
        out_specs=VMEM,
        compiler_params=PARAMS,
    )(parts)


def start_copies(pairs, sems):
    copies = [pltpu.make_async_copy(src, dst, sems.at[i]) for i, (src, dst) in enumerate(pairs)]
    for copy in copies:
        copy.start()
    return copies


def before_kernel(
    enc_hbm, dec_hbm, w_hbm, q_hbm, og_ref, kv_ref,
    w_ref, q_ref, part_ref, mask_ref, pk_ref, pv_ref, sw_ref,
    enc_ref, dec_ref, sems, *, own,
):
    copies = start_copies(
        ((enc_hbm, enc_ref), (dec_hbm, dec_ref), (q_hbm, q_ref), (w_hbm, w_ref)), sems
    )
    rows = q_ref.shape[0]
    sec = lax.axis_index("sec")
    kv = kv_ref[...]
    swapped = swap_keys_values(kv, own)
    sw_ref[...] = swapped
    for copy in copies[:3]:
        copy.wait()
    pk_ref[...], pv_ref[...] = probabilities(q_ref[...], kv, swapped, enc_ref[sec], own)
    valid_rows = dec_ref[sec] - lax.axis_index("seq") * rows
    row = lax.broadcasted_iota(jnp.int32, (rows, DH), 0)
    mask_ref[...] = jnp.where(row < valid_rows, 1.0, 0.0)
    copies[3].wait()
    part_ref[...] = project(og_ref, w_ref, lax.axis_index("mc"))


def after_kernel(
    og_ref, kv_ref, w_ref, q_ref, part_ref, mask_ref, pk_ref, pv_ref, sw_ref, dq_ref, panel_ref, *, own
):
    grad = part_ref[...] + project(og_ref, w_ref, 1 - lax.axis_index("mc"))
    g = jnp.where(mask_ref[...] > 0.0, grad, 0.0).astype(BF16)
    gradients(
        g, q_ref[...], kv_ref[...], sw_ref[...], pk_ref[...], pv_ref[...], dq_ref, panel_ref, own
    )


def body(queries, keys_values, out_grad, out_weight, enc_len, dec_len):
    rows = queries.shape[0]
    own = keys_values.shape[1]
    groups = lax.axis_size("seq")
    total = 2 * own * groups
    kv = exchange(jnp.broadcast_to(keys_values[None], (groups, 2, own, DH)), KV_FIRST)
    kv = kv.reshape(total, DH)
    og, kv = lax.optimization_barrier((lax.all_gather(out_grad, "my", axis=0), kv))
    og_other = lax.ppermute(og, "mc", [(0, 1), (1, 0)])
    kept = pl.pallas_call(
        lambda *refs: before_kernel(*refs, own=own),
        name="softmax_and_own_columns",
        out_shape=(
            jax.ShapeDtypeStruct(out_weight.shape, BF16),
            jax.ShapeDtypeStruct((rows, DH), BF16),
            jax.ShapeDtypeStruct((rows, DH), F32),
            jax.ShapeDtypeStruct((rows, DH), F32),
            jax.ShapeDtypeStruct((rows, total), F32),
            jax.ShapeDtypeStruct((rows, total), BF16),
            jax.ShapeDtypeStruct((total, DH), BF16),
        ),
        in_specs=[HBM] * 4 + [VMEM] * 2,
        out_specs=(VMEM,) * 7,
        scratch_shapes=[
            pltpu.SMEM(enc_len.shape, jnp.int32),
            pltpu.SMEM(dec_len.shape, jnp.int32),
            pltpu.SemaphoreType.DMA((4,)),
        ],
        compiler_params=PARAMS,
    )(*map(in_hbm, (enc_len, dec_len, out_weight, queries)), og, kv)
    query_grad, panel = pl.pallas_call(
        lambda *refs: after_kernel(*refs, own=own),
        name="gradients",
        out_shape=(
            jax.ShapeDtypeStruct((rows, DH), BF16),
            jax.ShapeDtypeStruct((total, DH), BF16),
        ),
        in_specs=[VMEM] * 9,
        out_specs=(VMEM, VMEM),
        compiler_params=PARAMS,
    )(og_other, kv, *kept)
    return query_grad, sum_over_seq(panel, groups, own)


def solution(mesh):
    sizes = dict(mesh.shape)
    fine = Mesh(
        mesh.devices.reshape(sizes["sec"], sizes["seq"], sizes["mp"] // 2, 2),
        ("sec", "seq", "my", "mc"),
    )
    tok, mp = ("sec", "seq"), ("my", "mc")
    return jax.shard_map(
        body,
        mesh=fine,
        in_specs=(P(tok, mp), P(None, tok, mp), P(tok, mp), P(mp, None), P(), P()),
        out_specs=(P(tok, mp), P(None, tok, mp)),
        check_vma=False,
    )
```

```python
import jax
import jax.numpy as jnp
from jax import lax
from jax.experimental import pallas as pl
from jax.experimental.pallas import tpu as pltpu
from jax.sharding import Mesh, PartitionSpec as P

DH = 256
F32 = jnp.float32
BF16 = jnp.bfloat16
VMEM = pl.BlockSpec(memory_space=pltpu.VMEM)
HBM = pl.BlockSpec(memory_space=pltpu.HBM)
PARAMS = pltpu.CompilerParams(vmem_limit_bytes=32 * 1024 * 1024)
KV_FIRST = 24
SUM_FIRST = 30
CHIP_FIRST = 0


def dot_nt(a, b):
    return lax.dot_general(a, b, (((1,), (1,)), ((), ())), preferred_element_type=F32)


def dot_tn(a, b):
    return lax.dot_general(a, b, (((0,), (0,)), ((), ())), preferred_element_type=F32)


def masked_softmax(scores, allowed):
    scores = jnp.where(allowed, scores, -1e30)
    expo = jnp.where(allowed, jnp.exp(scores - jnp.max(scores, axis=1, keepdims=True)), 0.0)
    return expo / jnp.sum(expo, axis=1, keepdims=True)


def project(og_ref, w_ref, core):
    chips, rows, slab = og_ref.shape
    total = jnp.zeros((rows, DH), F32)
    for chip in range(chips):
        holder = (chip + CHIP_FIRST) % chips
        first = pl.multiple_of((2 * holder + core) * slab, slab)
        total += dot_nt(og_ref[chip], w_ref[:, pl.ds(first, slab)])
    return total


def swap_matrix(total, own):
    r = lax.broadcasted_iota(jnp.int32, (total, total), 0)
    c = lax.broadcasted_iota(jnp.int32, (total, total), 1)
    partner = jnp.where((r % (2 * own)) < own, r + own, r - own)
    return jnp.where(c == partner, 1.0, 0.0).astype(BF16)


def probabilities(q, kv, swap, enc_limit, own):
    rows, total = q.shape[0], kv.shape[0]
    peers = total // (2 * own)
    scale = DH ** (-0.5)
    col = lax.broadcasted_iota(jnp.int32, (rows, total), 1)
    is_key = (col % (2 * own)) < own
    peer = (col // (2 * own) + KV_FIRST) % peers
    inside = peer * own + col % own < enc_limit
    at_keys = masked_softmax(dot_nt(q, kv) * scale, is_key & inside)
    at_values = jnp.dot(at_keys.astype(BF16), swap, preferred_element_type=F32)
    return at_keys, at_values.astype(BF16)


def gradients(g, q, kv, swapped, prob, prob_v, dq_ref, panel_ref, own):
    scale = DH ** (-0.5)
    grad_prob = dot_nt(g, swapped)
    delta = jnp.sum(prob * grad_prob, axis=1, keepdims=True)
    grad_score = (prob * (grad_prob - delta)).astype(BF16)
    panel = dot_tn(grad_score, q) * scale + dot_tn(prob_v, g)
    peers = panel.shape[0] // (2 * own)
    shift = ((SUM_FIRST - KV_FIRST) % peers) * 2 * own
    if shift:
        panel = jnp.concatenate([panel[shift:], panel[:shift]], axis=0)
    panel_ref[...] = panel.astype(BF16)
    dq_ref[...] = (jnp.dot(grad_score, kv, preferred_element_type=F32) * scale).astype(BF16)


def sum_kernel(parts_ref, out_ref):
    total = jnp.sum(parts_ref[...].astype(F32), axis=0).astype(BF16)
    own = out_ref.shape[1]
    out_ref[0] = total[:own]
    out_ref[1] = total[own:]


def in_hbm(x):
    return pltpu.with_memory_space_constraint(x, pltpu.HBM)


def exchange(x, first):
    peers = x.shape[0]
    order = [(first + i) % peers for i in range(peers)]
    return lax.all_to_all(x, "seq", 0, 0, tiled=True, axis_index_groups=[order])


def gather_chips(x):
    chips = lax.axis_size("my")
    order = [(CHIP_FIRST + i) % chips for i in range(chips)]
    return lax.all_gather(x, "my", axis=0, axis_index_groups=[order])


def opening_kernel(
    enc_hbm, dec_hbm, kv_hbm, w_hbm, q_hbm, copies_hbm, w_ref, q_ref, mask_ref, limit_ref,
    enc_ref, dec_ref, kv_ref, copies_ref, sems,
):
    copies = start_copies(
        ((kv_hbm, kv_ref), (enc_hbm, enc_ref), (dec_hbm, dec_ref), (w_hbm, w_ref), (q_hbm, q_ref)),
        sems,
    )
    own = kv_ref.shape[1]
    copies[0].wait()
    for half in range(2):
        copies_ref[:, half * own : (half + 1) * own] = jnp.broadcast_to(
            kv_ref[half][None], (copies_ref.shape[0], own, DH)
        )
    out = pltpu.make_async_copy(copies_ref, copies_hbm, sems.at[5])
    out.start()
    copies[1].wait()
    copies[2].wait()
    sec = lax.axis_index("sec")
    limit_ref[...] = jnp.full(limit_ref.shape, enc_ref[sec], jnp.int32)
    valid_rows = dec_ref[sec] - lax.axis_index("seq") * q_ref.shape[0]
    row = lax.broadcasted_iota(jnp.int32, mask_ref.shape, 0)
    mask_ref[...] = jnp.where(row < valid_rows, 1.0, 0.0)
    copies[3].wait()
    copies[4].wait()
    out.wait()


def sum_over_seq(panel, groups, own):
    parts = exchange(panel.reshape(groups, 2 * own, DH), SUM_FIRST)
    return pl.pallas_call(
        sum_kernel,
        name="sum_of_parts",
        out_shape=jax.ShapeDtypeStruct((2, own, DH), BF16),
        in_specs=[VMEM],
        out_specs=VMEM,
        compiler_params=PARAMS,
    )(parts)


def start_copies(pairs, sems):
    copies = [pltpu.make_async_copy(src, dst, sems.at[i]) for i, (src, dst) in enumerate(pairs)]
    for copy in copies:
        copy.start()
    return copies


def before_kernel(
    limit_ref, w_ref, q_ref, og_ref, kv_ref, part_ref, pk_ref, pv_ref, sw_ref, *, own
):
    kv = kv_ref[...]
    swap = swap_matrix(kv.shape[0], own)
    pk_ref[...], pv_ref[...] = probabilities(q_ref[...], kv, swap, limit_ref[0:1, 0:1], own)
    sw_ref[...] = jnp.dot(swap, kv, preferred_element_type=F32).astype(BF16)
    part_ref[...] = project(og_ref, w_ref, lax.axis_index("mc"))


def after_kernel(
    og_ref, kv_ref, w_ref, q_ref, mask_ref, part_ref, pk_ref, pv_ref, sw_ref, dq_ref, panel_ref, *, own
):
    grad = part_ref[...] + project(og_ref, w_ref, 1 - lax.axis_index("mc"))
    g = jnp.where(mask_ref[...] > 0.0, grad, 0.0).astype(BF16)
    gradients(
        g, q_ref[...], kv_ref[...], sw_ref[...], pk_ref[...], pv_ref[...], dq_ref, panel_ref, own
    )


def body(queries, keys_values, out_grad, out_weight, enc_len, dec_len):
    rows = queries.shape[0]
    own = keys_values.shape[1]
    groups = lax.axis_size("seq")
    total = 2 * own * groups
    copies, w, q, mask, limit = pl.pallas_call(
        opening_kernel,
        name="kv_copies_and_loads",
        out_shape=(
            jax.ShapeDtypeStruct((groups, 2 * own, DH), BF16),
            jax.ShapeDtypeStruct(out_weight.shape, BF16),
            jax.ShapeDtypeStruct((rows, DH), BF16),
            jax.ShapeDtypeStruct((rows, DH), F32),
            jax.ShapeDtypeStruct((8, 128), jnp.int32),
        ),
        in_specs=[HBM] * 5,
        out_specs=(HBM,) + (VMEM,) * 4,
        scratch_shapes=[
            pltpu.SMEM(enc_len.shape, jnp.int32),
            pltpu.SMEM(dec_len.shape, jnp.int32),
            pltpu.VMEM(keys_values.shape, BF16),
            pltpu.VMEM((groups, 2 * own, DH), BF16),
            pltpu.SemaphoreType.DMA((6,)),
        ],
        compiler_params=PARAMS,
    )(*map(in_hbm, (enc_len, dec_len, keys_values, out_weight, queries)))
    kv = exchange(copies, KV_FIRST)
    kv = kv.reshape(total, DH)
    og, kv = lax.optimization_barrier((gather_chips(out_grad), kv))
    og_other = lax.ppermute(og, "mc", [(0, 1), (1, 0)])
    kept = pl.pallas_call(
        lambda *refs: before_kernel(*refs, own=own),
        name="softmax_and_own_columns",
        out_shape=(
            jax.ShapeDtypeStruct((rows, DH), F32),
            jax.ShapeDtypeStruct((rows, total), F32),
            jax.ShapeDtypeStruct((rows, total), BF16),
            jax.ShapeDtypeStruct((total, DH), BF16),
        ),
        in_specs=[VMEM] * 5,
        out_specs=(VMEM,) * 4,
        compiler_params=PARAMS,
    )(limit, w, q, og, kv)
    query_grad, panel = pl.pallas_call(
        lambda *refs: after_kernel(*refs, own=own),
        name="gradients",
        out_shape=(
            jax.ShapeDtypeStruct((rows, DH), BF16),
            jax.ShapeDtypeStruct((total, DH), BF16),
        ),
        in_specs=[VMEM] * 9,
        out_specs=(VMEM, VMEM),
        compiler_params=PARAMS,
    )(og_other, kv, w, q, mask, *kept)
    return query_grad, sum_over_seq(panel, groups, own)


def solution(mesh):
    sizes = dict(mesh.shape)
    fine = Mesh(
        mesh.devices.reshape(sizes["sec"], sizes["seq"], sizes["mp"] // 2, 2),
        ("sec", "seq", "my", "mc"),
    )
    tok, mp = ("sec", "seq"), ("my", "mc")
    return jax.shard_map(
        body,
        mesh=fine,
        in_specs=(P(tok, mp), P(None, tok, mp), P(tok, mp), P(mp, None), P(), P()),
        out_specs=(P(tok, mp), P(None, tok, mp)),
        check_vma=False,
    )
```

```python
import jax
import jax.numpy as jnp
from jax import lax
from jax.experimental import pallas as pl
from jax.experimental.pallas import tpu as pltpu
from jax.sharding import Mesh, PartitionSpec as P

DH = 256
F32 = jnp.float32
BF16 = jnp.bfloat16
VMEM = pl.BlockSpec(memory_space=pltpu.VMEM)
HBM = pl.BlockSpec(memory_space=pltpu.HBM)
PARAMS = pltpu.CompilerParams(vmem_limit_bytes=32 * 1024 * 1024)
KV_FIRST = 24
SUM_FIRST = 30
CHIP_FIRST = 0


def dot_nt(a, b):
    return lax.dot_general(a, b, (((1,), (1,)), ((), ())), preferred_element_type=F32)


def dot_tn(a, b):
    return lax.dot_general(a, b, (((0,), (0,)), ((), ())), preferred_element_type=F32)


def masked_softmax(scores, allowed):
    scores = jnp.where(allowed, scores, -1e30)
    expo = jnp.where(allowed, jnp.exp(scores - jnp.max(scores, axis=1, keepdims=True)), 0.0)
    return expo / jnp.sum(expo, axis=1, keepdims=True)


def project(og_ref, w_ref, core):
    chips, rows, slab = og_ref.shape
    total = jnp.zeros((rows, DH), F32)
    for chip in range(chips):
        holder = (chip + CHIP_FIRST) % chips
        first = pl.multiple_of((2 * holder + core) * slab, slab)
        total += dot_nt(og_ref[chip], w_ref[:, pl.ds(first, slab)])
    return total


def swap_matrix(total, own):
    r = lax.broadcasted_iota(jnp.int32, (total, total), 0)
    c = lax.broadcasted_iota(jnp.int32, (total, total), 1)
    partner = jnp.where((r % (2 * own)) < own, r + own, r - own)
    return jnp.where(c == partner, 1.0, 0.0).astype(BF16)


def probabilities(q, kv, swap, enc_limit, own):
    rows, total = q.shape[0], kv.shape[0]
    peers = total // (2 * own)
    scale = DH ** (-0.5)
    col = lax.broadcasted_iota(jnp.int32, (rows, total), 1)
    is_key = (col % (2 * own)) < own
    peer = (KV_FIRST + peers - col // (2 * own)) % peers
    inside = peer * own + col % own < enc_limit
    at_keys = masked_softmax(dot_nt(q, kv) * scale, is_key & inside)
    at_values = jnp.dot(at_keys.astype(BF16), swap, preferred_element_type=F32)
    return at_keys, at_values.astype(BF16)


def gradients(g, q, kv, swapped, prob, prob_v, dq_ref, panel_ref, own):
    scale = DH ** (-0.5)
    grad_prob = dot_nt(g, swapped)
    delta = jnp.sum(prob * grad_prob, axis=1, keepdims=True)
    grad_score = (prob * (grad_prob - delta)).astype(BF16)
    panel = dot_tn(grad_score, q) * scale + dot_tn(prob_v, g)
    peers = panel.shape[0] // (2 * own)
    shift = ((KV_FIRST - SUM_FIRST) % peers) * 2 * own
    if shift:
        panel = jnp.concatenate([panel[shift:], panel[:shift]], axis=0)
    panel_ref[...] = panel.astype(BF16)
    dq_ref[...] = (jnp.dot(grad_score, kv, preferred_element_type=F32) * scale).astype(BF16)


def sum_kernel(parts_ref, out_ref):
    total = jnp.sum(parts_ref[...].astype(F32), axis=0).astype(BF16)
    own = out_ref.shape[1]
    out_ref[0] = total[:own]
    out_ref[1] = total[own:]


def in_hbm(x):
    return pltpu.with_memory_space_constraint(x, pltpu.HBM)


def exchange(x, first):
    peers = x.shape[0]
    order = [(first - i) % peers for i in range(peers)]
    return lax.all_to_all(x, "seq", 0, 0, tiled=True, axis_index_groups=[order])


def gather_chips(x):
    chips = lax.axis_size("my")
    order = [(CHIP_FIRST + i) % chips for i in range(chips)]
    return lax.all_gather(x, "my", axis=0, axis_index_groups=[order])


def opening_kernel(
    enc_hbm, dec_hbm, kv_hbm, w_hbm, q_hbm, copies_hbm, w_ref, q_ref, mask_ref, limit_ref,
    enc_ref, dec_ref, kv_ref, copies_ref, sems,
):
    copies = start_copies(
        ((kv_hbm, kv_ref), (enc_hbm, enc_ref), (dec_hbm, dec_ref), (w_hbm, w_ref), (q_hbm, q_ref)),
        sems,
    )
    own = kv_ref.shape[1]
    copies[0].wait()
    for half in range(2):
        copies_ref[:, half * own : (half + 1) * own] = jnp.broadcast_to(
            kv_ref[half][None], (copies_ref.shape[0], own, DH)
        )
    out = pltpu.make_async_copy(copies_ref, copies_hbm, sems.at[5])
    out.start()
    copies[1].wait()
    copies[2].wait()
    sec = lax.axis_index("sec")
    limit_ref[...] = jnp.full(limit_ref.shape, enc_ref[sec], jnp.int32)
    valid_rows = dec_ref[sec] - lax.axis_index("seq") * q_ref.shape[0]
    row = lax.broadcasted_iota(jnp.int32, mask_ref.shape, 0)
    mask_ref[...] = jnp.where(row < valid_rows, 1.0, 0.0)
    copies[3].wait()
    copies[4].wait()
    out.wait()


def sum_over_seq(panel, groups, own):
    parts = exchange(panel.reshape(groups, 2 * own, DH), SUM_FIRST)
    return pl.pallas_call(
        sum_kernel,
        name="sum_of_parts",
        out_shape=jax.ShapeDtypeStruct((2, own, DH), BF16),
        in_specs=[VMEM],
        out_specs=VMEM,
        compiler_params=PARAMS,
    )(parts)


def start_copies(pairs, sems):
    copies = [pltpu.make_async_copy(src, dst, sems.at[i]) for i, (src, dst) in enumerate(pairs)]
    for copy in copies:
        copy.start()
    return copies


def before_kernel(
    limit_ref, w_ref, q_ref, og_ref, kv_ref, part_ref, pk_ref, pv_ref, sw_ref, *, own
):
    kv = kv_ref[...]
    swap = swap_matrix(kv.shape[0], own)
    pk_ref[...], pv_ref[...] = probabilities(q_ref[...], kv, swap, limit_ref[0:1, 0:1], own)
    sw_ref[...] = jnp.dot(swap, kv, preferred_element_type=F32).astype(BF16)
    part_ref[...] = project(og_ref, w_ref, lax.axis_index("mc"))


def after_kernel(
    og_ref, kv_ref, w_ref, q_ref, mask_ref, part_ref, pk_ref, pv_ref, sw_ref, dq_ref, panel_ref, *, own
):
    grad = part_ref[...] + project(og_ref, w_ref, 1 - lax.axis_index("mc"))
    g = jnp.where(mask_ref[...] > 0.0, grad, 0.0).astype(BF16)
    gradients(
        g, q_ref[...], kv_ref[...], sw_ref[...], pk_ref[...], pv_ref[...], dq_ref, panel_ref, own
    )


def body(queries, keys_values, out_grad, out_weight, enc_len, dec_len):
    rows = queries.shape[0]
    own = keys_values.shape[1]
    groups = lax.axis_size("seq")
    total = 2 * own * groups
    copies, w, q, mask, limit = pl.pallas_call(
        opening_kernel,
        name="kv_copies_and_loads",
        out_shape=(
            jax.ShapeDtypeStruct((groups, 2 * own, DH), BF16),
            jax.ShapeDtypeStruct(out_weight.shape, BF16),
            jax.ShapeDtypeStruct((rows, DH), BF16),
            jax.ShapeDtypeStruct((rows, DH), F32),
            jax.ShapeDtypeStruct((8, 128), jnp.int32),
        ),
        in_specs=[HBM] * 5,
        out_specs=(HBM,) + (VMEM,) * 4,
        scratch_shapes=[
            pltpu.SMEM(enc_len.shape, jnp.int32),
            pltpu.SMEM(dec_len.shape, jnp.int32),
            pltpu.VMEM(keys_values.shape, BF16),
            pltpu.VMEM((groups, 2 * own, DH), BF16),
            pltpu.SemaphoreType.DMA((6,)),
        ],
        compiler_params=PARAMS,
    )(*map(in_hbm, (enc_len, dec_len, keys_values, out_weight, queries)))
    kv = exchange(copies, KV_FIRST)
    kv = kv.reshape(total, DH)
    og, kv = lax.optimization_barrier((gather_chips(out_grad), kv))
    og_other = lax.ppermute(og, "mc", [(0, 1), (1, 0)])
    kept = pl.pallas_call(
        lambda *refs: before_kernel(*refs, own=own),
        name="softmax_and_own_columns",
        out_shape=(
            jax.ShapeDtypeStruct((rows, DH), F32),
            jax.ShapeDtypeStruct((rows, total), F32),
            jax.ShapeDtypeStruct((rows, total), BF16),
            jax.ShapeDtypeStruct((total, DH), BF16),
        ),
        in_specs=[VMEM] * 5,
        out_specs=(VMEM,) * 4,
        compiler_params=PARAMS,
    )(limit, w, q, og, kv)
    query_grad, panel = pl.pallas_call(
        lambda *refs: after_kernel(*refs, own=own),
        name="gradients",
        out_shape=(
            jax.ShapeDtypeStruct((rows, DH), BF16),
            jax.ShapeDtypeStruct((total, DH), BF16),
        ),
        in_specs=[VMEM] * 9,
        out_specs=(VMEM, VMEM),
        compiler_params=PARAMS,
    )(og_other, kv, w, q, mask, *kept)
    return query_grad, sum_over_seq(panel, groups, own)


def solution(mesh):
    sizes = dict(mesh.shape)
    fine = Mesh(
        mesh.devices.reshape(sizes["sec"], sizes["seq"], sizes["mp"] // 2, 2),
        ("sec", "seq", "my", "mc"),
    )
    tok, mp = ("sec", "seq"), ("my", "mc")
    return jax.shard_map(
        body,
        mesh=fine,
        in_specs=(P(tok, mp), P(None, tok, mp), P(tok, mp), P(mp, None), P(), P()),
        out_specs=(P(tok, mp), P(None, tok, mp)),
        check_vma=False,
    )
```

```python
import jax
import jax.numpy as jnp
from jax import lax
from jax.experimental import pallas as pl
from jax.experimental.pallas import tpu as pltpu
from jax.sharding import Mesh, PartitionSpec as P

DH = 256
F32 = jnp.float32
BF16 = jnp.bfloat16
VMEM = pl.BlockSpec(memory_space=pltpu.VMEM)
HBM = pl.BlockSpec(memory_space=pltpu.HBM)
PARAMS = pltpu.CompilerParams(vmem_limit_bytes=32 * 1024 * 1024)
KV_FIRST = 35
SUM_FIRST = 30
CHIP_FIRST = 0


def dot_nt(a, b):
    return lax.dot_general(a, b, (((1,), (1,)), ((), ())), preferred_element_type=F32)


def dot_tn(a, b):
    return lax.dot_general(a, b, (((0,), (0,)), ((), ())), preferred_element_type=F32)


def masked_softmax(scores, allowed):
    scores = jnp.where(allowed, scores, -1e30)
    expo = jnp.where(allowed, jnp.exp(scores - jnp.max(scores, axis=1, keepdims=True)), 0.0)
    return expo / jnp.sum(expo, axis=1, keepdims=True)


def project(og_ref, w_ref, core):
    chips, rows, slab = og_ref.shape
    total = jnp.zeros((rows, DH), F32)
    for chip in range(chips):
        holder = (chip + CHIP_FIRST) % chips
        first = pl.multiple_of((2 * holder + core) * slab, slab)
        total += dot_nt(og_ref[chip], w_ref[:, pl.ds(first, slab)])
    return total


def swap_matrix(total, own):
    r = lax.broadcasted_iota(jnp.int32, (total, total), 0)
    c = lax.broadcasted_iota(jnp.int32, (total, total), 1)
    partner = jnp.where((r % (2 * own)) < own, r + own, r - own)
    return jnp.where(c == partner, 1.0, 0.0).astype(BF16)


def probabilities(q, kv, swap, enc_limit, own):
    rows, total = q.shape[0], kv.shape[0]
    peers = total // (2 * own)
    scale = DH ** (-0.5)
    col = lax.broadcasted_iota(jnp.int32, (rows, total), 1)
    is_key = (col % (2 * own)) < own
    peer = (col // (2 * own) + KV_FIRST) % peers
    inside = peer * own + col % own < enc_limit
    at_keys = masked_softmax(dot_nt(q, kv) * scale, is_key & inside)
    at_values = jnp.dot(at_keys.astype(BF16), swap, preferred_element_type=F32)
    return at_keys, at_values.astype(BF16)


def gradients(g, q, kv, swapped, prob, prob_v, dq_ref, panel_ref, own):
    scale = DH ** (-0.5)
    grad_prob = dot_nt(g, swapped)
    delta = jnp.sum(prob * grad_prob, axis=1, keepdims=True)
    grad_score = (prob * (grad_prob - delta)).astype(BF16)
    panel = dot_tn(grad_score, q) * scale + dot_tn(prob_v, g)
    peers = panel.shape[0] // (2 * own)
    shift = ((SUM_FIRST - KV_FIRST) % peers) * 2 * own
    if shift:
        panel = jnp.concatenate([panel[shift:], panel[:shift]], axis=0)
    panel_ref[...] = panel.astype(BF16)
    dq_ref[...] = (jnp.dot(grad_score, kv, preferred_element_type=F32) * scale).astype(BF16)


def sum_kernel(parts_ref, out_ref):
    total = jnp.sum(parts_ref[...].astype(F32), axis=0).astype(BF16)
    own = out_ref.shape[1]
    out_ref[0] = total[:own]
    out_ref[1] = total[own:]


def in_hbm(x):
    return pltpu.with_memory_space_constraint(x, pltpu.HBM)


def exchange(x, first):
    peers = x.shape[0]
    order = [(first + i) % peers for i in range(peers)]
    return lax.all_to_all(x, "seq", 0, 0, tiled=True, axis_index_groups=[order])


def gather_chips(x):
    chips = lax.axis_size("my")
    order = [(CHIP_FIRST + i) % chips for i in range(chips)]
    return lax.all_gather(x, "my", axis=0, axis_index_groups=[order])


def opening_kernel(
    enc_hbm, dec_hbm, kv_hbm, w_hbm, q_hbm, copies_hbm, w_ref, q_ref, mask_ref, limit_ref,
    enc_ref, dec_ref, kv_ref, copies_ref, sems,
):
    copies = start_copies(
        ((kv_hbm, kv_ref), (enc_hbm, enc_ref), (dec_hbm, dec_ref), (w_hbm, w_ref), (q_hbm, q_ref)),
        sems,
    )
    own = kv_ref.shape[1]
    copies[0].wait()
    for half in range(2):
        copies_ref[:, half * own : (half + 1) * own] = jnp.broadcast_to(
            kv_ref[half][None], (copies_ref.shape[0], own, DH)
        )
    out = pltpu.make_async_copy(copies_ref, copies_hbm, sems.at[5])
    out.start()
    copies[1].wait()
    copies[2].wait()
    sec = lax.axis_index("sec")
    limit_ref[...] = jnp.full(limit_ref.shape, enc_ref[sec], jnp.int32)
    valid_rows = dec_ref[sec] - lax.axis_index("seq") * q_ref.shape[0]
    row = lax.broadcasted_iota(jnp.int32, mask_ref.shape, 0)
    mask_ref[...] = jnp.where(row < valid_rows, 1.0, 0.0)
    copies[3].wait()
    copies[4].wait()
    out.wait()


def sum_over_seq(panel, groups, own):
    parts = exchange(panel.reshape(groups, 2 * own, DH), SUM_FIRST)
    return pl.pallas_call(
        sum_kernel,
        name="sum_of_parts",
        out_shape=jax.ShapeDtypeStruct((2, own, DH), BF16),
        in_specs=[VMEM],
        out_specs=VMEM,
        compiler_params=PARAMS,
    )(parts)


def start_copies(pairs, sems):
    copies = [pltpu.make_async_copy(src, dst, sems.at[i]) for i, (src, dst) in enumerate(pairs)]
    for copy in copies:
        copy.start()
    return copies


def before_kernel(
    limit_ref, w_ref, q_ref, og_ref, kv_ref, part_ref, pk_ref, pv_ref, sw_ref, *, own
):
    kv = kv_ref[...]
    swap = swap_matrix(kv.shape[0], own)
    pk_ref[...], pv_ref[...] = probabilities(q_ref[...], kv, swap, limit_ref[0:1, 0:1], own)
    sw_ref[...] = jnp.dot(swap, kv, preferred_element_type=F32).astype(BF16)
    part_ref[...] = project(og_ref, w_ref, lax.axis_index("mc"))


def after_kernel(
    og_ref, kv_ref, w_ref, q_ref, mask_ref, part_ref, pk_ref, pv_ref, sw_ref, dq_ref, panel_ref, *, own
):
    grad = part_ref[...] + project(og_ref, w_ref, 1 - lax.axis_index("mc"))
    g = jnp.where(mask_ref[...] > 0.0, grad, 0.0).astype(BF16)
    gradients(
        g, q_ref[...], kv_ref[...], sw_ref[...], pk_ref[...], pv_ref[...], dq_ref, panel_ref, own
    )


def body(queries, keys_values, out_grad, out_weight, enc_len, dec_len):
    rows = queries.shape[0]
    own = keys_values.shape[1]
    groups = lax.axis_size("seq")
    total = 2 * own * groups
    copies, w, q, mask, limit = pl.pallas_call(
        opening_kernel,
        name="kv_copies_and_loads",
        out_shape=(
            jax.ShapeDtypeStruct((groups, 2 * own, DH), BF16),
            jax.ShapeDtypeStruct(out_weight.shape, BF16),
            jax.ShapeDtypeStruct((rows, DH), BF16),
            jax.ShapeDtypeStruct((rows, DH), F32),
            jax.ShapeDtypeStruct((8, 128), jnp.int32),
        ),
        in_specs=[HBM] * 5,
        out_specs=(HBM,) + (VMEM,) * 4,
        scratch_shapes=[
            pltpu.SMEM(enc_len.shape, jnp.int32),
            pltpu.SMEM(dec_len.shape, jnp.int32),
            pltpu.VMEM(keys_values.shape, BF16),
            pltpu.VMEM((groups, 2 * own, DH), BF16),
            pltpu.SemaphoreType.DMA((6,)),
        ],
        compiler_params=PARAMS,
    )(*map(in_hbm, (enc_len, dec_len, keys_values, out_weight, queries)))
    kv = exchange(copies, KV_FIRST)
    kv = kv.reshape(total, DH)
    og, kv = lax.optimization_barrier((gather_chips(out_grad), kv))
    og_other = lax.ppermute(og, "mc", [(0, 1), (1, 0)])
    kept = pl.pallas_call(
        lambda *refs: before_kernel(*refs, own=own),
        name="softmax_and_own_columns",
        out_shape=(
            jax.ShapeDtypeStruct((rows, DH), F32),
            jax.ShapeDtypeStruct((rows, total), F32),
            jax.ShapeDtypeStruct((rows, total), BF16),
            jax.ShapeDtypeStruct((total, DH), BF16),
        ),
        in_specs=[VMEM] * 5,
        out_specs=(VMEM,) * 4,
        compiler_params=PARAMS,
    )(limit, w, q, og, kv)
    query_grad, panel = pl.pallas_call(
        lambda *refs: after_kernel(*refs, own=own),
        name="gradients",
        out_shape=(
            jax.ShapeDtypeStruct((rows, DH), BF16),
            jax.ShapeDtypeStruct((total, DH), BF16),
        ),
        in_specs=[VMEM] * 9,
        out_specs=(VMEM, VMEM),
        compiler_params=PARAMS,
    )(og_other, kv, w, q, mask, *kept)
    return query_grad, sum_over_seq(panel, groups, own)


def solution(mesh):
    sizes = dict(mesh.shape)
    fine = Mesh(
        mesh.devices.reshape(sizes["sec"], sizes["seq"], sizes["mp"] // 2, 2),
        ("sec", "seq", "my", "mc"),
    )
    tok, mp = ("sec", "seq"), ("my", "mc")
    return jax.shard_map(
        body,
        mesh=fine,
        in_specs=(P(tok, mp), P(None, tok, mp), P(tok, mp), P(mp, None), P(), P()),
        out_specs=(P(tok, mp), P(None, tok, mp)),
        check_vma=False,
    )
```
